32 devices in a mesh: ctx: 8 (over y, x, core), head: 4 (over z).
Axes of the slice: x: 2, y: 2, z: 4, core: 2. Of those that a mesh axis runs over, the one named last changes fastest.
Arguments:
- query_low: bfloat16 [2, 1536], P(None, 'ctx'), may hold values from -6 to 6
- query_weight: bfloat16 [1536, 73728], P('ctx', 'head'), may hold values from -0.21875 to 0.21875
- latent_cache: bfloat16 [2, 32768, 576], P(None, ('ctx', 'head')), may hold values from -300 to 300
- lengths: int32 [2], replicated, may hold values from 20481 to 32768
- value_weight: bfloat16 [128, 512, 128], P('head'), may hold values from -2 to 2
- output_weight: bfloat16 [16384, 7168], P('head', 'ctx'), may hold values from -0.0625 to 0.0625
Outputs:
- attended: bfloat16 [2, 7168], P(None, ('ctx', 'head'))
The draws below stay inside these ranges and needn't reach their ends.
All inputs are finite; a program needn't handle non-finite values.
Results may differ from the reference program's by a relative error of at most 0.028.
Values may be sent and summed in bfloat16 or wider, within the bound.
A program may use at most 192 MiB of HBM per device.

```python
import jax
import jax.numpy as jnp
from jax import lax

D = 7168
HEADS = 128
QL = 1536
KV_RANK = 512
ROPE_DIM = 64
V_DIM = 128
SEQS = 2
CTX_DEV = 1024
LENGTH = 32768


def draw_latent_cache(key, part):
    width = KV_RANK + ROPE_DIM

    def one_sequence(sequence):
        row_key = jax.random.fold_in(key, sequence)
        common = jnp.clip(jax.random.normal(jax.random.fold_in(row_key, 11), (KV_RANK,), jnp.float32), -3.0, 3.0)
        fraction = jnp.arange(LENGTH, dtype=jnp.float32) / LENGTH
        values = jnp.clip(jax.random.normal(row_key, (LENGTH, width), jnp.float32), -6.0, 6.0)
        ramp = 3.0 * fraction - 1.0
        latent = values[:, :KV_RANK] + ramp[:, None] * common[None, :]
        values = jnp.concatenate([latent, values[:, KV_RANK:]], axis=1)
        return values.astype(jnp.bfloat16)
    return lax.map(one_sequence, jnp.arange(SEQS))


def spiked(array, stream_key, source, target, blocks, factor):
    def block_of(dim):
        return (jnp.arange(array.shape[dim]) // (array.shape[dim] // blocks)).reshape((-1,) + (1,) * (array.ndim - 1 - dim))

    one_side = jax.random.permutation(stream_key, blocks)[block_of(target)]
    second = (block_of(target) + blocks // 2) % blocks
    return jnp.where((block_of(source) == one_side) | (block_of(source) == second), factor * array, array)


def block_scale(key, extent, split, low, largest):
    gain, own = 1.0, jax.random.fold_in(key, 6)
    for axis_at, blocks in split:
        steps = jnp.exp(jax.random.uniform(jax.random.fold_in(own, axis_at), (blocks,), jnp.float32, low / len(split), largest / len(split)))
        gain = gain * jnp.repeat(steps, extent[axis_at] // blocks).reshape([-1 if axis == axis_at else 1 for axis in range(len(extent))])
    return gain


def normal_values(stream_key, extent, deviation, reach, shards=(), kind=jnp.bfloat16):
    factor_of = block_scale(stream_key, extent, shards, -0.22, 0.18) if shards else 1.0
    result = jax.random.normal(stream_key, extent, jnp.float32) * deviation * factor_of
    return jnp.minimum(jnp.maximum(result, -reach), reach).astype(kind)


def noise_with(own_key, shape, deviation, limit, shards, heavy, kind=jnp.bfloat16):
    drawn = deviation * jax.random.normal(own_key, shape, jnp.float32)
    if shards:
        drawn = drawn * block_scale(own_key, shape, shards, -0.22, 0.18)
    return jnp.clip(spiked(drawn, jax.random.fold_in(own_key, 3), *heavy), -limit, limit).astype(kind)


def setup_inputs(seed: int = 0) -> dict:
    seeds = jax.random.split(jax.random.key(seed), 7)
    query_low = normal_values(seeds[0], (SEQS, QL), 1.0, 6.0, ((1, 8),))
    query_weight = normal_values(seeds[1], (QL, HEADS * (KV_RANK + ROPE_DIM)), (QL // 2) ** -0.5, 0.21875, ((0, 8), (1, 4)))
    latent_cache = draw_latent_cache(jax.random.fold_in(seeds[6], 71), 0)
    lengths = jax.random.randint(seeds[3], (SEQS,), LENGTH * 5 // 8 + 1, LENGTH + 1).astype(jnp.int32)
    value_weight = normal_values(seeds[4], (HEADS, KV_RANK, V_DIM), (KV_RANK // 64) ** -0.5, 2.0, ((0, 4),))
    output_weight = noise_with(seeds[5], (HEADS * V_DIM, D), (HEADS * V_DIM) ** -0.5, 0.0625, ((0, 4), (1, 8)), (0, 1, 8, 2.0))
    return {"query_low": query_low, "query_weight": query_weight, "latent_cache": latent_cache, "lengths": lengths, "value_weight": value_weight, "output_weight": output_weight}


softmax_scale = 0.07216878


def reference(query_low, query_weight, latent_cache, lengths, value_weight, output_weight):
    sequences = query_low.shape[0]
    head_count = value_weight.shape[0]
    rounded = jnp.dot(query_low, query_weight, preferred_element_type=jnp.float32).astype(jnp.bfloat16)
    queries = lax.optimization_barrier(rounded).reshape(sequences, head_count, -1).astype(jnp.float32)
    block_count = LENGTH // CTX_DEV

    def advance(running, block_index):
        maximum, totals, numerators = running
        offset = (block_index * CTX_DEV).astype(jnp.int32)
        pieces = lax.dynamic_slice_in_dim(latent_cache, offset, CTX_DEV, 1).astype(jnp.float32)
        scores = jnp.einsum("bhc,bpc->bhp", queries, pieces) * softmax_scale
        places = offset + jnp.arange(CTX_DEV, dtype=jnp.int32)
        usable = (places[None, :] < lengths[:, None])[:, None, :]
        scores = jnp.where(usable, scores, -1e30)
        block_max = jnp.max(scores, axis=2)
        probabilities = jnp.where(usable, jnp.exp(scores - block_max[..., None]), 0.0)
        block_total = jnp.sum(probabilities, axis=2)
        weights = lax.optimization_barrier(probabilities.astype(jnp.bfloat16)).astype(jnp.float32)
        block_numerator = jnp.einsum("bhp,bpc->bhc", weights, pieces[:, :, :KV_RANK])
        highest = jnp.maximum(maximum, block_max)
        old_scale = jnp.exp(maximum - highest)
        new_scale = jnp.exp(block_max - highest)
        totals = totals * old_scale + block_total * new_scale
        numerators = numerators * old_scale[..., None] + block_numerator * new_scale[..., None]
        return (highest, totals, numerators), None

    start_state = (jnp.full((sequences, head_count), -1e30, jnp.float32),
                   jnp.zeros((sequences, head_count), jnp.float32),
                   jnp.zeros((sequences, head_count, KV_RANK), jnp.float32))
    final_state, _ = lax.scan(advance, start_state, jnp.arange(block_count, dtype=jnp.int32))
    latent_out = (final_state[2] / final_state[1][..., None]).astype(jnp.bfloat16)
    values = jnp.einsum("bhc,hcv->bhv", latent_out.astype(jnp.float32), value_weight.astype(jnp.float32)).astype(jnp.bfloat16)
    return jnp.dot(values.reshape(sequences, -1), output_weight, preferred_element_type=jnp.float32).astype(jnp.bfloat16)
```

```python
import functools

import jax
import jax.numpy as jnp
from jax import lax
from jax.experimental import pallas as pl
from jax.experimental.pallas import tpu as pltpu
from jax.sharding import PartitionSpec as P

softmax_scale = 0.07216878
LANES = 128
F32 = jnp.float32
BF16 = jnp.bfloat16


def parts_of(x):
    high = x.astype(BF16).astype(F32)
    rest = x - high
    middle = rest.astype(BF16).astype(F32)
    return high, middle, rest - middle


def lane_sum(x, first, last):
    lane = lax.broadcasted_iota(jnp.int32, x.shape, x.ndim - 1)
    return jnp.sum(jnp.where((lane >= first) & (lane < last), x, 0.0), axis=-1, keepdims=True)


def kernel(
    ctx_count,
    head_count,
    lengths,
    query_low,
    query_weight,
    latent_cache,
    value_weight,
    output_weight,
    out,
    qw,
    cache,
    vw,
    ow,
    partial,
    partial_in,
    summed,
    query_rows,
    gathered,
    queries,
    numer,
    stat_rows,
    stat_send,
    stat_in,
    plane_send,
    plane_in,
    value_rows,
    value_all,
    projected,
    out_send,
    out_in,
    load_sem,
    qw_sem,
    p_send,
    p_recv,
    gz_send,
    gz_recv,
    gc_send,
    gc_recv,
    s_send,
    s_recv,
    z_send,
    z_recv,
    v_send,
    v_recv,
    o_send,
    o_recv,
):
    C, H = ctx_count, head_count
    me_c, me_h = lax.axis_index("ctx"), lax.axis_index("head")
    sequences = query_low.shape[0]
    pieces, depth, _ = qw.shape
    chunk = partial.shape[2]
    rows = query_rows.shape[0]
    own_heads = rows // sequences
    span, width = cache.shape[1], cache.shape[2]
    rank = vw.shape[1]
    v_dim = vw.shape[2]
    share = out.shape[1]

    def ctx_peer(step):
        return lax.rem(me_c + step, C)

    def head_peer(step):
        return lax.rem(me_h + step, H)

    def remote(source, target, send_sem, recv_sem, c, h):
        return pltpu.make_async_remote_copy(
            src_ref=source,
            dst_ref=target,
            send_sem=send_sem,
            recv_sem=recv_sem,
            device_id=(c, h),
            device_id_type=pl.DeviceIdType.MESH,
        )

    def loop(low, high, body):
        def run(i, carry):
            body(i)
            return carry

        lax.fori_loop(low, high, run, 0)

    def qw_copy(index):
        if pieces == 1:
            return pltpu.make_async_copy(query_weight, qw.at[0], qw_sem.at[0])
        columns = pl.ds(pl.multiple_of(index * chunk, LANES), chunk)
        return pltpu.make_async_copy(query_weight.at[:, columns], qw.at[index], qw_sem.at[index])

    if pieces == 1:
        qw_copy(0).start()
    else:
        loop(1, C + 1, lambda o: qw_copy(ctx_peer(o)).start())
    barrier = pltpu.get_barrier_semaphore()

    def greet(c, h):
        pl.semaphore_signal(
            barrier, inc=1, device_id=(c, h), device_id_type=pl.DeviceIdType.MESH
        )

    loop(1, C, lambda o: greet(ctx_peer(o), me_h))
    loop(1, H, lambda o: greet(me_c, head_peer(o)))
    cache_copy = pltpu.make_async_copy(latent_cache, cache, load_sem.at[0])
    cache_copy.start()
    vw_copy = pltpu.make_async_copy(
        value_weight.at[pl.ds(me_c * own_heads, own_heads)], vw, load_sem.at[1]
    )
    vw_copy.start()
    ow_copy = pltpu.make_async_copy(output_weight, ow, load_sem.at[2])
    ow_copy.start()
    pl.semaphore_wait(barrier, C + H - 2)

    def p_copy(o):
        c = ctx_peer(o)
        return remote(
            partial.at[c], partial_in.at[me_c], p_send.at[o], p_recv.at[me_c], c, me_h
        )

    def multiply(index):
        qw_copy(index).wait()
        partial[index] = jnp.dot(query_low[...], qw[index], preferred_element_type=F32)

    if pieces == 1:
        qw_copy(0).wait()
        for c in range(C):
            partial[c] = jnp.dot(
                query_low[...], qw[0, :, c * chunk : (c + 1) * chunk], preferred_element_type=F32
            )
        loop(1, C, lambda o: p_copy(o).start())
    else:

        def send_partial(o):
            multiply(ctx_peer(o))
            p_copy(o).start()

        loop(1, C, send_partial)
        multiply(me_c)
    query_rows[...] = jnp.zeros_like(query_rows)
    partial_in[me_c] = partial[me_c]

    def p_wait(o):
        c = ctx_peer(o)
        remote(partial.at[c], partial_in.at[c], p_send.at[o], p_recv.at[c], c, me_h).wait_recv()

    loop(1, C, p_wait)
    total = partial_in[0]
    for c in range(1, C):
        total = total + partial_in[c]
    summed[...] = total
    for b in range(sequences):
        for j in range(own_heads):
            row = b * own_heads + j
            query_rows[row : row + 1, 0:width] = summed[b : b + 1, j * width : (j + 1) * width]
    gathered[me_h, me_c] = query_rows[...].astype(BF16)

    def gz_copy(o):
        h = head_peer(o)
        slot = gathered.at[me_h, me_c]
        return remote(slot, slot, gz_send.at[o], gz_recv.at[me_h], me_c, h)

    def gc_copy(step, o):
        h = head_peer(step)
        slot = gathered.at[h, me_c]
        return remote(slot, slot, gc_send.at[step, o], gc_recv.at[h, me_c], ctx_peer(o), me_h)

    loop(1, H, lambda o: gz_copy(o).start())
    loop(1, C, lambda o: gc_copy(0, o).start())

    def forward(step):
        h = head_peer(step)
        slot = gathered.at[h, me_c]
        remote(slot, slot, gz_send.at[step], gz_recv.at[h], me_c, h).wait_recv()
        loop(1, C, lambda o: gc_copy(step, o).start())

    loop(1, H, forward)

    def gc_wait(step):
        def one(o):
            h, c = head_peer(step), ctx_peer(o)
            slot = gathered.at[h, c]
            remote(slot, slot, gc_send.at[step, o], gc_recv.at[h, c], c, me_h).wait_recv()

        loop(1, C, one)

    cache_copy.wait()
    loop(0, H, gc_wait)
    for h in range(H):
        for c in range(C):
            block = gathered[h, c].astype(F32)
            first = (h * C + c) * own_heads
            for b in range(sequences):
                queries[b, first : first + own_heads, :] = block[
                    b * own_heads : (b + 1) * own_heads, :
                ]

    offset = (me_c * H + me_h) * span
    all_heads = queries.shape[1]
    for b in range(sequences):
        usable = (
            offset + lax.broadcasted_iota(jnp.int32, (all_heads, span), 1)
        ) < lengths[b]
        scores = (
            lax.dot_general(
                queries[b, :, 0:width].astype(BF16),
                cache[b],
                (((1,), (1,)), ((), ())),
                preferred_element_type=F32,
            )
            * softmax_scale
        )
        scores = jnp.where(usable, scores, -1e30)
        local_max = jnp.max(scores, axis=1, keepdims=True)
        probabilities = jnp.where(usable, jnp.exp(scores - local_max), 0.0)
        totals = jnp.sum(probabilities, axis=1, keepdims=True)
        numer[b, :, 0:rank] = jnp.dot(
            probabilities.astype(BF16), cache[b, :, 0:rank], preferred_element_type=F32
        )
        lane = lax.broadcasted_iota(jnp.int32, (all_heads, LANES), 1)
        extra = jnp.zeros((all_heads, LANES), F32)
        for at, part in enumerate(parts_of(local_max) + parts_of(totals)):
            extra = jnp.where(lane == at, part, extra)
        numer[b, :, rank:] = extra
    for h in range(H):
        for c in range(C):
            first = (h * C + c) * own_heads
            for b in range(sequences):
                stat_rows[c, h, b * own_heads : (b + 1) * own_heads, :] = numer[
                    b, first : first + own_heads, :
                ]
    stat_send[...] = stat_rows[...].astype(BF16)

    def s_copy(o):
        c = ctx_peer(o)
        return remote(stat_send.at[c], stat_in.at[me_c], s_send.at[o], s_recv.at[me_c], c, me_h)

    loop(1, C, lambda o: s_copy(o).start())
    stat_in[me_c] = stat_send[me_c]

    def s_wait(o):
        c = ctx_peer(o)
        remote(stat_send.at[c], stat_in.at[c], s_send.at[o], s_recv.at[c], c, me_h).wait_recv()

    loop(1, C, s_wait)
    maxima, sums = [], []
    for c in range(C):
        extra = stat_in[c, :, :, rank:].astype(F32)
        maxima.append(lane_sum(extra, 0, 3))
        sums.append(lane_sum(extra, 3, 6))
    highest = functools.reduce(jnp.maximum, maxima)
    total, weighted = 0.0, 0.0
    for c in range(C):
        scale = jnp.exp(maxima[c] - highest)
        total = total + sums[c] * scale
        weighted = weighted + stat_in[c, :, :, 0:rank].astype(F32) * scale
    lane = lax.broadcasted_iota(jnp.int32, (H, rows, LANES), 2)
    plane_send[:, :, 0:rank] = weighted
    plane_send[:, :, rank:] = jnp.where(lane == 0, highest, jnp.where(lane == 1, total, 0.0))

    def z_copy(o):
        h = head_peer(o)
        return remote(plane_send.at[h], plane_in.at[me_h], z_send.at[o], z_recv.at[me_h], me_c, h)

    loop(1, H, lambda o: z_copy(o).start())
    plane_in[me_h] = plane_send[me_h]

    def z_wait(o):
        h = head_peer(o)
        remote(plane_send.at[h], plane_in.at[h], z_send.at[o], z_recv.at[h], me_c, h).wait_recv()

    loop(1, H, z_wait)
    maxima, sums = [], []
    for h in range(H):
        extra = plane_in[h, :, rank:]
        maxima.append(lane_sum(extra, 0, 1))
        sums.append(lane_sum(extra, 1, 2))
    highest = functools.reduce(jnp.maximum, maxima)
    total, weighted = 0.0, 0.0
    for h in range(H):
        scale = jnp.exp(maxima[h] - highest)
        total = total + sums[h] * scale
        weighted = weighted + plane_in[h, :, 0:rank] * scale
    latent_out = (weighted / total).astype(BF16)

    vw_copy.wait()
    for j in range(own_heads):
        value = jnp.dot(latent_out, vw[j], preferred_element_type=F32)
        for b in range(sequences):
            row = b * own_heads + j
            value_rows[b : b + 1, j * v_dim : (j + 1) * v_dim] = value[row : row + 1, :]
    value_all[me_c] = value_rows[...].astype(BF16)

    def v_copy(o):
        slot = value_all.at[me_c]
        return remote(slot, slot, v_send.at[o], v_recv.at[me_c], ctx_peer(o), me_h)

    loop(1, C, lambda o: v_copy(o).start())

    def v_wait(o):
        c = ctx_peer(o)
        slot = value_all.at[c]
        remote(slot, slot, v_send.at[o], v_recv.at[c], c, me_h).wait_recv()

    ow_copy.wait()
    loop(1, C, v_wait)
    block_rows = own_heads * v_dim
    projected[...] = jnp.zeros_like(projected)

    def project(c):
        at = pl.ds(pl.multiple_of(c * block_rows, block_rows), block_rows)
        projected[...] += jnp.dot(value_all[c], ow[at, :], preferred_element_type=F32)

    loop(0, C, project)
    for h in range(H):
        out_send[h] = projected[:, h * share : (h + 1) * share]

    def o_copy(o):
        h = head_peer(o)
        return remote(out_send.at[h], out_in.at[me_h], o_send.at[o], o_recv.at[me_h], me_c, h)

    loop(1, H, lambda o: o_copy(o).start())
    out_in[me_h] = out_send[me_h]

    def o_wait(o):
        h = head_peer(o)
        remote(out_send.at[h], out_in.at[h], o_send.at[o], o_recv.at[h], me_c, h).wait_recv()

    loop(1, H, o_wait)
    result = out_in[0]
    for h in range(1, H):
        result = result + out_in[h]
    out[...] = result

    loop(1, C, lambda o: p_copy(o).wait_send())
    loop(1, H, lambda o: gz_copy(o).wait_send())
    loop(0, H, lambda step: loop(1, C, lambda o: gc_copy(step, o).wait_send()))
    loop(1, C, lambda o: s_copy(o).wait_send())
    loop(1, H, lambda o: z_copy(o).wait_send())
    loop(1, C, lambda o: v_copy(o).wait_send())
    loop(1, H, lambda o: o_copy(o).wait_send())


def on_device(
    C, H, query_low, query_weight, latent_cache, lengths, value_weight, output_weight
):
    sequences = query_low.shape[0]
    local_heads, rank, v_dim = value_weight.shape
    _, span, width = latent_cache.shape
    depth, columns = query_weight.shape
    own_heads = local_heads // C
    chunk = columns // C
    rows = sequences * own_heads
    all_heads = local_heads * H
    padded = rank + LANES
    features = output_weight.shape[1]
    share = features // H
    qw_shape = (C, depth, chunk) if chunk % LANES == 0 else (1, depth, columns)
    vmem, dma = pltpu.VMEM, pltpu.SemaphoreType.DMA
    result = pl.pallas_call(
        functools.partial(kernel, C, H),
        out_shape=jax.ShapeDtypeStruct((sequences, share), F32),
        in_specs=[
            pl.BlockSpec(memory_space=pltpu.SMEM),
            pl.BlockSpec(memory_space=pltpu.VMEM),
            pl.BlockSpec(memory_space=pl.ANY),
            pl.BlockSpec(memory_space=pl.ANY),
            pl.BlockSpec(memory_space=pl.ANY),
            pl.BlockSpec(memory_space=pl.ANY),
        ],
        out_specs=pl.BlockSpec(memory_space=pltpu.VMEM),
        scratch_shapes=[
            vmem(qw_shape, BF16),
            vmem(latent_cache.shape, BF16),
            vmem((own_heads, rank, v_dim), BF16),
            vmem(output_weight.shape, BF16),
            vmem((C, sequences, chunk), F32),
            vmem((C, sequences, chunk), F32),
            vmem((sequences, chunk), F32),
            vmem((rows, padded), F32),
            vmem((H, C, rows, padded), BF16),
            vmem((sequences, all_heads, padded), F32),
            vmem((sequences, all_heads, padded), F32),
            vmem((C, H, rows, padded), F32),
            vmem((C, H, rows, padded), BF16),
            vmem((C, H, rows, padded), BF16),
            vmem((H, rows, padded), F32),
            vmem((H, rows, padded), F32),
            vmem((sequences, own_heads * v_dim), F32),
            vmem((C, sequences, own_heads * v_dim), BF16),
            vmem((sequences, features), F32),
            vmem((H, sequences, share), F32),
            vmem((H, sequences, share), F32),
            dma((3,)),
            dma((C,)),
            dma((C,)),
            dma((C,)),
            dma((H,)),
            dma((H,)),
            dma((H, C)),
            dma((H, C)),
            dma((C,)),
            dma((C,)),
            dma((H,)),
            dma((H,)),
            dma((C,)),
            dma((C,)),
            dma((H,)),
            dma((H,)),
        ],
        compiler_params=pltpu.CompilerParams(
            collective_id=0, has_side_effects=True, vmem_limit_bytes=48 * 1024 * 1024
        ),
    )(lengths, query_low, query_weight, latent_cache, value_weight, output_weight)
    return result.astype(BF16)


def solution(mesh):
    return jax.shard_map(
        functools.partial(on_device, mesh.shape["ctx"], mesh.shape["head"]),
        mesh=mesh,
        in_specs=(
            P(None, "ctx"),
            P("ctx", "head"),
            P(None, ("ctx", "head"), None),
            P(),
            P("head", None, None),
            P("head", "ctx"),
        ),
        out_specs=P(None, ("ctx", "head")),
        check_vma=False,
    )
```

```python
import functools

import jax
import jax.numpy as jnp
from jax import lax
from jax.experimental import pallas as pl
from jax.experimental.pallas import tpu as pltpu
from jax.sharding import PartitionSpec as P

softmax_scale = 0.07216878
LANES = 128
F32 = jnp.float32
BF16 = jnp.bfloat16


def parts_of(x):
    high = x.astype(BF16).astype(F32)
    rest = x - high
    middle = rest.astype(BF16).astype(F32)
    return high, middle, rest - middle


def lane_sum(x, first, last):
    lane = lax.broadcasted_iota(jnp.int32, x.shape, x.ndim - 1)
    return jnp.sum(jnp.where((lane >= first) & (lane < last), x, 0.0), axis=-1, keepdims=True)


def kernel(
    ctx_count,
    head_count,
    lengths,
    query_low,
    query_weight,
    latent_cache,
    value_weight,
    output_weight,
    out,
    qw,
    cache,
    vw,
    ow,
    partial,
    partial_in,
    summed,
    query_rows,
    gathered,
    queries,
    numer,
    latent_rows,
    stat_send,
    stat_in,
    plane_send,
    plane_in,
    value_rows,
    value_all,
    projected,
    out_send,
    out_in,
    load_sem,
    qw_sem,
    p_send,
    p_recv,
    gz_send,
    gz_recv,
    gc_send,
    gc_recv,
    s_send,
    s_recv,
    z_send,
    z_recv,
    v_send,
    v_recv,
    o_send,
    o_recv,
):
    C, H = ctx_count, head_count
    me_c, me_h = lax.axis_index("ctx"), lax.axis_index("head")
    sequences = query_low.shape[0]
    pieces, depth, _ = qw.shape
    chunk = partial.shape[2]
    own_heads = query_rows.shape[1]
    width, span = cache.shape[1], cache.shape[2]
    rank = vw.shape[1]
    v_dim = vw.shape[2]
    share = out.shape[1]

    def ctx_peer(step):
        return lax.rem(me_c + step, C)

    def head_peer(step):
        return lax.rem(me_h + step, H)

    def remote(source, target, send_sem, recv_sem, c, h):
        return pltpu.make_async_remote_copy(
            src_ref=source,
            dst_ref=target,
            send_sem=send_sem,
            recv_sem=recv_sem,
            device_id=(c, h),
            device_id_type=pl.DeviceIdType.MESH,
        )

    def loop(low, high, body):
        def run(i, carry):
            body(i)
            return carry

        lax.fori_loop(low, high, run, 0)

    def qw_copy(index):
        if pieces == 1:
            return pltpu.make_async_copy(query_weight, qw.at[0], qw_sem.at[0])
        columns = pl.ds(pl.multiple_of(index * chunk, LANES), chunk)
        return pltpu.make_async_copy(query_weight.at[:, columns], qw.at[index], qw_sem.at[index])

    if pieces == 1:
        qw_copy(0).start()
    else:
        loop(1, C + 1, lambda o: qw_copy(ctx_peer(o)).start())
    barrier = pltpu.get_barrier_semaphore()

    def greet(c, h):
        pl.semaphore_signal(
            barrier, inc=1, device_id=(c, h), device_id_type=pl.DeviceIdType.MESH
        )

    loop(1, C, lambda o: greet(ctx_peer(o), me_h))
    loop(1, H, lambda o: greet(me_c, head_peer(o)))
    cache_copy = pltpu.make_async_copy(latent_cache, cache, load_sem.at[0])
    vw_copy = pltpu.make_async_copy(
        value_weight.at[pl.ds(me_c * own_heads, own_heads)], vw, load_sem.at[1]
    )
    ow_copy = pltpu.make_async_copy(output_weight, ow, load_sem.at[2])

    def p_copy(o):
        c = ctx_peer(o)
        return remote(
            partial.at[c], partial_in.at[me_c], p_send.at[o], p_recv.at[me_c], c, me_h
        )

    def multiply(index):
        qw_copy(index).wait()
        partial[index] = jnp.dot(query_low[...], qw[index], preferred_element_type=F32)

    if pieces == 1:
        qw_copy(0).wait()
        for c in range(C):
            partial[c] = jnp.dot(
                query_low[...], qw[0, :, c * chunk : (c + 1) * chunk], preferred_element_type=F32
            )
        pl.semaphore_wait(barrier, C + H - 2)
        loop(1, C, lambda o: p_copy(o).start())
    else:

        def send_partial(o):
            p_copy(o).start()
            multiply(ctx_peer(o + 1))

        multiply(ctx_peer(1))
        pl.semaphore_wait(barrier, C + H - 2)
        loop(1, C, send_partial)
    cache_copy.start()
    vw_copy.start()
    ow_copy.start()
    query_rows[...] = jnp.zeros_like(query_rows)
    partial_in[me_c] = partial[me_c]

    def p_wait(o):
        c = ctx_peer(o)
        remote(partial.at[c], partial_in.at[c], p_send.at[o], p_recv.at[c], c, me_h).wait_recv()

    loop(1, C, p_wait)
    total = partial_in[0]
    for c in range(1, C):
        total = total + partial_in[c]
    summed[...] = total
    for b in range(sequences):
        for j in range(own_heads):
            query_rows[b, j : j + 1, 0:width] = summed[b : b + 1, j * width : (j + 1) * width]
        gathered[b, me_h, me_c] = query_rows[b].astype(BF16)

    def gz_copy(b, o):
        h = head_peer(o)
        slot = gathered.at[b, me_h, me_c]
        return remote(slot, slot, gz_send.at[b, o], gz_recv.at[b, me_h], me_c, h)

    def gc_copy(b, step, o):
        h = head_peer(step)
        slot = gathered.at[b, h, me_c]
        return remote(
            slot, slot, gc_send.at[b, step, o], gc_recv.at[b, h, me_c], ctx_peer(o), me_h
        )

    def forward(b, step):
        h = head_peer(step)
        slot = gathered.at[b, h, me_c]
        remote(slot, slot, gz_send.at[b, step], gz_recv.at[b, h], me_c, h).wait_recv()
        loop(1, C, lambda o: gc_copy(b, step, o).start())

    def gc_wait(b, step):
        def one(o):
            h, c = head_peer(step), ctx_peer(o)
            slot = gathered.at[b, h, c]
            remote(slot, slot, gc_send.at[b, step, o], gc_recv.at[b, h, c], c, me_h).wait_recv()

        loop(1, C, one)

    for b in range(sequences):
        loop(1, H, lambda o: gz_copy(b, o).start())
        loop(1, C, lambda o: gc_copy(b, 0, o).start())
    for b in range(sequences):
        loop(1, H, lambda step: forward(b, step))
    cache_copy.wait()

    def s_copy(b, o):
        c = ctx_peer(o)
        return remote(
            stat_send.at[b, c], stat_in.at[b, me_c], s_send.at[b, o], s_recv.at[b, me_c], c, me_h
        )

    offset = (me_c * H + me_h) * span
    all_heads = queries.shape[1]
    for b in range(sequences):
        loop(0, H, lambda step: gc_wait(b, step))
        for h in range(H):
            for c in range(C):
                first = (h * C + c) * own_heads
                queries[b, first : first + own_heads, :] = gathered[b, h, c].astype(F32)
        usable = (
            offset + lax.broadcasted_iota(jnp.int32, (all_heads, span), 1)
        ) < lengths[b]
        scores = (
            jnp.dot(
                queries[b, :, 0:width].astype(BF16), cache[b], preferred_element_type=F32
            )
            * softmax_scale
        )
        scores = jnp.where(usable, scores, -1e30)
        local_max = jnp.max(scores, axis=1, keepdims=True)
        probabilities = jnp.where(usable, jnp.exp(scores - local_max), 0.0)
        totals = jnp.sum(probabilities, axis=1, keepdims=True)
        numer[b, :, 0:rank] = lax.dot_general(
            probabilities.astype(BF16),
            cache[b, 0:rank, :],
            (((1,), (1,)), ((), ())),
            preferred_element_type=F32,
        )
        lane = lax.broadcasted_iota(jnp.int32, (all_heads, LANES), 1)
        extra = jnp.zeros((all_heads, LANES), F32)
        for at, part in enumerate(parts_of(local_max) + parts_of(totals)):
            extra = jnp.where(lane == at, part, extra)
        numer[b, :, rank:] = extra
        for h in range(H):
            for c in range(C):
                first = (h * C + c) * own_heads
                stat_send[b, c, h] = numer[b, first : first + own_heads, :].astype(BF16)
        loop(1, C, lambda o: s_copy(b, o).start())
        stat_in[b, me_c] = stat_send[b, me_c]

    def s_wait(b, o):
        c = ctx_peer(o)
        remote(
            stat_send.at[b, c], stat_in.at[b, c], s_send.at[b, o], s_recv.at[b, c], c, me_h
        ).wait_recv()

    def z_copy(b, o):
        h = head_peer(o)
        return remote(
            plane_send.at[b, h], plane_in.at[b, me_h], z_send.at[b, o], z_recv.at[b, me_h], me_c, h
        )

    def z_wait(b, o):
        h = head_peer(o)
        remote(
            plane_send.at[b, h], plane_in.at[b, h], z_send.at[b, o], z_recv.at[b, h], me_c, h
        ).wait_recv()

    for b in range(sequences):
        loop(1, C, lambda o: s_wait(b, o))
        maxima, sums = [], []
        for c in range(C):
            extra = stat_in[b, c, :, :, rank:].astype(F32)
            maxima.append(lane_sum(extra, 0, 3))
            sums.append(lane_sum(extra, 3, 6))
        highest = functools.reduce(jnp.maximum, maxima)
        total, weighted = 0.0, 0.0
        for c in range(C):
            scale = jnp.exp(maxima[c] - highest)
            total = total + sums[c] * scale
            weighted = weighted + stat_in[b, c, :, :, 0:rank].astype(F32) * scale
        lane = lax.broadcasted_iota(jnp.int32, (H, own_heads, LANES), 2)
        plane_send[b, :, :, 0:rank] = weighted
        plane_send[b, :, :, rank:] = jnp.where(
            lane == 0, highest, jnp.where(lane == 1, total, 0.0)
        )
        loop(1, H, lambda o: z_copy(b, o).start())
        plane_in[b, me_h] = plane_send[b, me_h]
    for b in range(sequences):
        loop(1, H, lambda o: z_wait(b, o))
        maxima, sums = [], []
        for h in range(H):
            extra = plane_in[b, h, :, rank:]
            maxima.append(lane_sum(extra, 0, 1))
            sums.append(lane_sum(extra, 1, 2))
        highest = functools.reduce(jnp.maximum, maxima)
        total, weighted = 0.0, 0.0
        for h in range(H):
            scale = jnp.exp(maxima[h] - highest)
            total = total + sums[h] * scale
            weighted = weighted + plane_in[b, h, :, 0:rank] * scale
        latent_rows[b * own_heads : (b + 1) * own_heads, :] = weighted / total
    latent_out = latent_rows[...].astype(BF16)

    vw_copy.wait()
    for j in range(own_heads):
        value = jnp.dot(latent_out, vw[j], preferred_element_type=F32)
        for b in range(sequences):
            row = b * own_heads + j
            value_rows[b : b + 1, j * v_dim : (j + 1) * v_dim] = value[row : row + 1, :]
    value_all[me_c] = value_rows[...].astype(BF16)

    def v_copy(o):
        slot = value_all.at[me_c]
        return remote(slot, slot, v_send.at[o], v_recv.at[me_c], ctx_peer(o), me_h)

    loop(1, C, lambda o: v_copy(o).start())

    def v_wait(o):
        c = ctx_peer(o)
        slot = value_all.at[c]
        remote(slot, slot, v_send.at[o], v_recv.at[c], c, me_h).wait_recv()

    ow_copy.wait()
    block_rows = own_heads * v_dim
    projected[...] = jnp.zeros_like(projected)

    def project(c):
        at = pl.ds(pl.multiple_of(c * block_rows, block_rows), block_rows)
        projected[...] += jnp.dot(value_all[c], ow[at, :], preferred_element_type=F32)

    def project_next(o):
        v_wait(o)
        project(ctx_peer(o))

    project(me_c)
    loop(1, C, project_next)
    for h in range(H):
        out_send[h] = projected[:, h * share : (h + 1) * share]

    def o_copy(o):
        h = head_peer(o)
        return remote(out_send.at[h], out_in.at[me_h], o_send.at[o], o_recv.at[me_h], me_c, h)

    loop(1, H, lambda o: o_copy(o).start())
    out_in[me_h] = out_send[me_h]

    def o_wait(o):
        h = head_peer(o)
        remote(out_send.at[h], out_in.at[h], o_send.at[o], o_recv.at[h], me_c, h).wait_recv()

    loop(1, H, o_wait)
    result = out_in[0]
    for h in range(1, H):
        result = result + out_in[h]
    out[...] = result

    loop(1, C, lambda o: p_copy(o).wait_send())
    for b in range(sequences):
        loop(1, H, lambda o: gz_copy(b, o).wait_send())
        loop(0, H, lambda step: loop(1, C, lambda o: gc_copy(b, step, o).wait_send()))
        loop(1, C, lambda o: s_copy(b, o).wait_send())
        loop(1, H, lambda o: z_copy(b, o).wait_send())
    loop(1, C, lambda o: v_copy(o).wait_send())
    loop(1, H, lambda o: o_copy(o).wait_send())


def on_device(
    C, H, query_low, query_weight, latent_cache, lengths, value_weight, output_weight
):
    latent_cache = jnp.swapaxes(latent_cache, 1, 2)
    sequences = query_low.shape[0]
    local_heads, rank, v_dim = value_weight.shape
    depth, columns = query_weight.shape
    own_heads = local_heads // C
    chunk = columns // C
    all_heads = local_heads * H
    padded = rank + LANES
    features = output_weight.shape[1]
    share = features // H
    qw_shape = (C, depth, chunk) if chunk % LANES == 0 else (1, depth, columns)
    vmem, dma = pltpu.VMEM, pltpu.SemaphoreType.DMA
    result = pl.pallas_call(
        functools.partial(kernel, C, H),
        out_shape=jax.ShapeDtypeStruct((sequences, share), F32),
        in_specs=[
            pl.BlockSpec(memory_space=pltpu.SMEM),
            pl.BlockSpec(memory_space=pltpu.VMEM),
            pl.BlockSpec(memory_space=pl.ANY),
            pl.BlockSpec(memory_space=pl.ANY),
            pl.BlockSpec(memory_space=pl.ANY),
            pl.BlockSpec(memory_space=pl.ANY),
        ],
        out_specs=pl.BlockSpec(memory_space=pltpu.VMEM),
        scratch_shapes=[
            vmem(qw_shape, BF16),
            vmem(latent_cache.shape, BF16),
            vmem((own_heads, rank, v_dim), BF16),
            vmem(output_weight.shape, BF16),
            vmem((C, sequences, chunk), F32),
            vmem((C, sequences, chunk), F32),
            vmem((sequences, chunk), F32),
            vmem((sequences, own_heads, padded), F32),
            vmem((sequences, H, C, own_heads, padded), BF16),
            vmem((sequences, all_heads, padded), F32),
            vmem((sequences, all_heads, padded), F32),
            vmem((sequences * own_heads, rank), F32),
            vmem((sequences, C, H, own_heads, padded), BF16),
            vmem((sequences, C, H, own_heads, padded), BF16),
            vmem((sequences, H, own_heads, padded), F32),
            vmem((sequences, H, own_heads, padded), F32),
            vmem((sequences, own_heads * v_dim), F32),
            vmem((C, sequences, own_heads * v_dim), BF16),
            vmem((sequences, features), F32),
            vmem((H, sequences, share), F32),
            vmem((H, sequences, share), F32),
            dma((3,)),
            dma((C,)),
            dma((C,)),
            dma((C,)),
            dma((sequences, H)),
            dma((sequences, H)),
            dma((sequences, H, C)),
            dma((sequences, H, C)),
            dma((sequences, C)),
            dma((sequences, C)),
            dma((sequences, H)),
            dma((sequences, H)),
            dma((C,)),
            dma((C,)),
            dma((H,)),
            dma((H,)),
        ],
        compiler_params=pltpu.CompilerParams(
            collective_id=0, has_side_effects=True, vmem_limit_bytes=48 * 1024 * 1024
        ),
    )(lengths, query_low, query_weight, latent_cache, value_weight, output_weight)
    return result.astype(BF16)


def solution(mesh):
    return jax.shard_map(
        functools.partial(on_device, mesh.shape["ctx"], mesh.shape["head"]),
        mesh=mesh,
        in_specs=(
            P(None, "ctx"),
            P("ctx", "head"),
            P(None, ("ctx", "head"), None),
            P(),
            P("head", None, None),
            P("head", "ctx"),
        ),
        out_specs=P(None, ("ctx", "head")),
        check_vma=False,
    )
```

```python
import functools

import jax
import jax.numpy as jnp
from jax import lax
from jax.experimental import pallas as pl
from jax.experimental.pallas import tpu as pltpu
from jax.sharding import PartitionSpec as P

softmax_scale = 0.07216878
LANES = 128
F32 = jnp.float32
BF16 = jnp.bfloat16


def parts_of(x):
    high = x.astype(BF16).astype(F32)
    rest = x - high
    middle = rest.astype(BF16).astype(F32)
    return high, middle, rest - middle


def lane_sum(x, first, last):
    lane = lax.broadcasted_iota(jnp.int32, x.shape, x.ndim - 1)
    return jnp.sum(jnp.where((lane >= first) & (lane < last), x, 0.0), axis=-1, keepdims=True)


def kernel(
    ctx_count,
    head_count,
    lengths_from,
    query_low_from,
    query_weight,
    latent_cache,
    value_weight,
    output_weight,
    out,
    lengths,
    query_low,
    spread,
    qw,
    cache,
    vw,
    ow,
    partial,
    partial_in,
    summed,
    query_rows,
    gathered,
    queries,
    numer,
    latent_rows,
    stat_send,
    stat_in,
    plane_send,
    plane_in,
    value_rows,
    value_all,
    projected,
    out_send,
    out_in,
    load_sem,
    qw_sem,
    p_send,
    p_recv,
    gz_send,
    gz_recv,
    gc_send,
    gc_recv,
    s_send,
    s_recv,
    z_send,
    z_recv,
    v_send,
    v_recv,
    o_send,
    o_recv,
):
    C, H = ctx_count, head_count
    me_c, me_h = lax.axis_index("ctx"), lax.axis_index("head")
    sequences = query_low.shape[0]
    pieces, depth, _ = qw.shape
    chunk = partial.shape[2]
    own_heads = query_rows.shape[1]
    width, span = cache.shape[1], cache.shape[2]
    rank = vw.shape[1]
    v_dim = vw.shape[2]
    share = out.shape[1]

    def ctx_peer(step):
        return lax.rem(me_c + step, C)

    def head_peer(step):
        return lax.rem(me_h + step, H)

    def remote(source, target, send_sem, recv_sem, c, h):
        return pltpu.make_async_remote_copy(
            src_ref=source,
            dst_ref=target,
            send_sem=send_sem,
            recv_sem=recv_sem,
            device_id=(c, h),
            device_id_type=pl.DeviceIdType.MESH,
        )

    def loop(low, high, body):
        def run(i, carry):
            body(i)
            return carry

        lax.fori_loop(low, high, run, 0)

    def qw_copy(index):
        if pieces == 1:
            return pltpu.make_async_copy(query_weight, qw.at[0], qw_sem.at[0])
        columns = pl.ds(pl.multiple_of(index * chunk, LANES), chunk)
        return pltpu.make_async_copy(query_weight.at[:, columns], qw.at[index], qw_sem.at[index])

    barrier = pltpu.get_barrier_semaphore()

    def greet(c, h):
        pl.semaphore_signal(
            barrier, inc=1, device_id=(c, h), device_id_type=pl.DeviceIdType.MESH
        )

    loop(1, H, lambda o: greet(me_c, head_peer(o)))
    loop(1, C, lambda o: greet(ctx_peer(o), me_h))

    lengths_copy = pltpu.make_async_copy(lengths_from, lengths, load_sem.at[3])
    low_copy = pltpu.make_async_copy(query_low_from, query_low, load_sem.at[4])
    low_copy.start()
    lengths_copy.start()
    if pieces == 1:
        qw_copy(0).start()
    else:
        loop(1, C + 1, lambda o: qw_copy(ctx_peer(o)).start())
    cache_copy = pltpu.make_async_copy(latent_cache, cache, load_sem.at[0])
    vw_copy = pltpu.make_async_copy(
        value_weight.at[pl.ds(me_c * own_heads, own_heads)], vw, load_sem.at[1]
    )
    ow_copy = pltpu.make_async_copy(output_weight, ow, load_sem.at[2])

    low_copy.wait()
    for b in range(sequences):
        pick = lax.broadcasted_iota(jnp.int32, (sequences, LANES), 0) == b
        spread[b] = lax.dot_general(
            query_low[...],
            jnp.where(pick, 1.0, 0.0).astype(BF16),
            (((0,), (0,)), ((), ())),
            preferred_element_type=F32,
        )

    def p_copy(o):
        c = ctx_peer(o)
        return remote(
            partial.at[c], partial_in.at[me_c], p_send.at[o], p_recv.at[me_c], c, me_h
        )

    def multiply(index):
        qw_copy(index).wait()
        for at in range(0, chunk, LANES):
            weight = qw[index, :, at : at + LANES].astype(F32)
            for b in range(sequences):
                partial[index, b : b + 1, at : at + LANES] = jnp.sum(
                    weight * spread[b], axis=0, keepdims=True
                )

    if pieces == 1:
        qw_copy(0).wait()
        for c in range(C):
            partial[c] = jnp.dot(
                query_low[...], qw[0, :, c * chunk : (c + 1) * chunk], preferred_element_type=F32
            )
        pl.semaphore_wait(barrier, C + H - 2)
        loop(1, C, lambda o: p_copy(o).start())
    else:

        def send_partial(o):
            p_copy(o).start()
            multiply(ctx_peer(o + 1))

        multiply(ctx_peer(1))
        pl.semaphore_wait(barrier, C + H - 2)
        loop(1, C, send_partial)
    cache_copy.start()
    vw_copy.start()
    ow_copy.start()
    query_rows[...] = jnp.zeros_like(query_rows)
    partial_in[me_c] = partial[me_c]

    def p_wait(o):
        c = ctx_peer(o)
        remote(partial.at[c], partial_in.at[c], p_send.at[o], p_recv.at[c], c, me_h).wait_recv()

    loop(1, C, p_wait)
    total = partial_in[0]
    for c in range(1, C):
        total = total + partial_in[c]
    summed[...] = total
    for b in range(sequences):
        for j in range(own_heads):
            query_rows[b, j : j + 1, 0:width] = summed[b : b + 1, j * width : (j + 1) * width]
        gathered[b, me_h, me_c] = query_rows[b].astype(BF16)

    def gz_copy(b, o):
        h = head_peer(o)
        slot = gathered.at[b, me_h, me_c]
        return remote(slot, slot, gz_send.at[b, o], gz_recv.at[b, me_h], me_c, h)

    def gc_copy(b, step, o):
        h = head_peer(step)
        slot = gathered.at[b, h, me_c]
        return remote(
            slot, slot, gc_send.at[b, step, o], gc_recv.at[b, h, me_c], ctx_peer(o), me_h
        )

    def forward(b, step):
        h = head_peer(step)
        slot = gathered.at[b, h, me_c]
        remote(slot, slot, gz_send.at[b, step], gz_recv.at[b, h], me_c, h).wait_recv()
        loop(1, C, lambda o: gc_copy(b, step, o).start())

    def gc_wait(b, step):
        def one(o):
            h, c = head_peer(step), ctx_peer(o)
            slot = gathered.at[b, h, c]
            remote(slot, slot, gc_send.at[b, step, o], gc_recv.at[b, h, c], c, me_h).wait_recv()

        loop(1, C, one)

    for b in range(sequences):
        loop(1, H, lambda o: gz_copy(b, o).start())
        loop(1, C, lambda o: gc_copy(b, 0, o).start())
    for b in range(sequences):
        loop(1, H, lambda step: forward(b, step))
    cache_copy.wait()

    def s_copy(b, o):
        c = ctx_peer(o)
        return remote(
            stat_send.at[b, c], stat_in.at[b, me_c], s_send.at[b, o], s_recv.at[b, me_c], c, me_h
        )

    lengths_copy.wait()
    offset = (me_c * H + me_h) * span
    all_heads = queries.shape[1]
    for b in range(sequences):
        loop(0, H, lambda step: gc_wait(b, step))
        for h in range(H):
            for c in range(C):
                first = (h * C + c) * own_heads
                queries[b, first : first + own_heads, :] = gathered[b, h, c].astype(F32)
        usable = (
            offset + lax.broadcasted_iota(jnp.int32, (all_heads, span), 1)
        ) < lengths[b]
        scores = (
            jnp.dot(
                queries[b, :, 0:width].astype(BF16), cache[b], preferred_element_type=F32
            )
            * softmax_scale
        )
        scores = jnp.where(usable, scores, -1e30)
        local_max = jnp.max(scores, axis=1, keepdims=True)
        probabilities = jnp.where(usable, jnp.exp(scores - local_max), 0.0)
        totals = jnp.sum(probabilities, axis=1, keepdims=True)
        numer[b, :, 0:rank] = lax.dot_general(
            probabilities.astype(BF16),
            cache[b, 0:rank, :],
            (((1,), (1,)), ((), ())),
            preferred_element_type=F32,
        )
        lane = lax.broadcasted_iota(jnp.int32, (all_heads, LANES), 1)
        extra = jnp.zeros((all_heads, LANES), F32)
        for at, part in enumerate(parts_of(local_max) + parts_of(totals)):
            extra = jnp.where(lane == at, part, extra)
        numer[b, :, rank:] = extra
        for h in range(H):
            for c in range(C):
                first = (h * C + c) * own_heads
                stat_send[b, c, h] = numer[b, first : first + own_heads, :].astype(BF16)
        loop(1, C, lambda o: s_copy(b, o).start())
        stat_in[b, me_c] = stat_send[b, me_c]

    def s_wait(b, o):
        c = ctx_peer(o)
        remote(
            stat_send.at[b, c], stat_in.at[b, c], s_send.at[b, o], s_recv.at[b, c], c, me_h
        ).wait_recv()

    def z_copy(b, o):
        h = head_peer(o)
        return remote(
            plane_send.at[b, h], plane_in.at[b, me_h], z_send.at[b, o], z_recv.at[b, me_h], me_c, h
        )

    def z_wait(b, o):
        h = head_peer(o)
        remote(
            plane_send.at[b, h], plane_in.at[b, h], z_send.at[b, o], z_recv.at[b, h], me_c, h
        ).wait_recv()

    for b in range(sequences):
        loop(1, C, lambda o: s_wait(b, o))
        maxima, sums = [], []
        for c in range(C):
            extra = stat_in[b, c, :, :, rank:].astype(F32)
            maxima.append(lane_sum(extra, 0, 3))
            sums.append(lane_sum(extra, 3, 6))
        highest = functools.reduce(jnp.maximum, maxima)
        total, weighted = 0.0, 0.0
        for c in range(C):
            scale = jnp.exp(maxima[c] - highest)
            total = total + sums[c] * scale
            weighted = weighted + stat_in[b, c, :, :, 0:rank].astype(F32) * scale
        lane = lax.broadcasted_iota(jnp.int32, (H, own_heads, LANES), 2)
        plane_send[b, :, :, 0:rank] = weighted
        plane_send[b, :, :, rank:] = jnp.where(
            lane == 0, highest, jnp.where(lane == 1, total, 0.0)
        )
        loop(1, H, lambda o: z_copy(b, o).start())
        plane_in[b, me_h] = plane_send[b, me_h]
    for b in range(sequences):
        loop(1, H, lambda o: z_wait(b, o))
        maxima, sums = [], []
        for h in range(H):
            extra = plane_in[b, h, :, rank:]
            maxima.append(lane_sum(extra, 0, 1))
            sums.append(lane_sum(extra, 1, 2))
        highest = functools.reduce(jnp.maximum, maxima)
        total, weighted = 0.0, 0.0
        for h in range(H):
            scale = jnp.exp(maxima[h] - highest)
            total = total + sums[h] * scale
            weighted = weighted + plane_in[b, h, :, 0:rank] * scale
        latent_rows[b * own_heads : (b + 1) * own_heads, :] = weighted / total
    latent_out = latent_rows[...].astype(BF16)

    vw_copy.wait()
    for j in range(own_heads):
        value = jnp.dot(latent_out, vw[j], preferred_element_type=F32)
        for b in range(sequences):
            row = b * own_heads + j
            value_rows[b : b + 1, j * v_dim : (j + 1) * v_dim] = value[row : row + 1, :]
    value_all[me_c] = value_rows[...].astype(BF16)

    def v_copy(o):
        slot = value_all.at[me_c]
        return remote(slot, slot, v_send.at[o], v_recv.at[me_c], ctx_peer(o), me_h)

    loop(1, C, lambda o: v_copy(o).start())

    def v_wait(o):
        c = ctx_peer(o)
        slot = value_all.at[c]
        remote(slot, slot, v_send.at[o], v_recv.at[c], c, me_h).wait_recv()

    ow_copy.wait()
    block_rows = own_heads * v_dim
    projected[...] = jnp.zeros_like(projected)

    def project(c):
        at = pl.ds(pl.multiple_of(c * block_rows, block_rows), block_rows)
        projected[...] += jnp.dot(value_all[c], ow[at, :], preferred_element_type=F32)

    def project_next(o):
        v_wait(o)
        project(ctx_peer(o))

    project(me_c)
    loop(1, C, project_next)
    for h in range(H):
        out_send[h] = projected[:, h * share : (h + 1) * share]

    def o_copy(o):
        h = head_peer(o)
        return remote(out_send.at[h], out_in.at[me_h], o_send.at[o], o_recv.at[me_h], me_c, h)

    loop(1, H, lambda o: o_copy(o).start())
    out_in[me_h] = out_send[me_h]

    def o_wait(o):
        h = head_peer(o)
        remote(out_send.at[h], out_in.at[h], o_send.at[o], o_recv.at[h], me_c, h).wait_recv()

    loop(1, H, o_wait)
    result = out_in[0]
    for h in range(1, H):
        result = result + out_in[h]
    out[...] = result

    loop(1, C, lambda o: p_copy(o).wait_send())
    for b in range(sequences):
        loop(1, H, lambda o: gz_copy(b, o).wait_send())
        loop(0, H, lambda step: loop(1, C, lambda o: gc_copy(b, step, o).wait_send()))
        loop(1, C, lambda o: s_copy(b, o).wait_send())
        loop(1, H, lambda o: z_copy(b, o).wait_send())
    loop(1, C, lambda o: v_copy(o).wait_send())
    loop(1, H, lambda o: o_copy(o).wait_send())


def on_device(
    C, H, query_low, query_weight, latent_cache, lengths, value_weight, output_weight
):
    latent_cache = jnp.swapaxes(latent_cache, 1, 2)
    sequences = query_low.shape[0]
    local_heads, rank, v_dim = value_weight.shape
    depth, columns = query_weight.shape
    own_heads = local_heads // C
    chunk = columns // C
    all_heads = local_heads * H
    padded = rank + LANES
    features = output_weight.shape[1]
    share = features // H
    qw_shape = (C, depth, chunk) if chunk % LANES == 0 else (1, depth, columns)
    vmem, dma = pltpu.VMEM, pltpu.SemaphoreType.DMA
    result = pl.pallas_call(
        functools.partial(kernel, C, H),
        out_shape=jax.ShapeDtypeStruct((sequences, share), F32),
        in_specs=[
            pl.BlockSpec(memory_space=pltpu.HBM),
            pl.BlockSpec(memory_space=pltpu.HBM),
            pl.BlockSpec(memory_space=pltpu.HBM),
            pl.BlockSpec(memory_space=pltpu.HBM),
            pl.BlockSpec(memory_space=pltpu.HBM),
            pl.BlockSpec(memory_space=pltpu.HBM),
        ],
        out_specs=pl.BlockSpec(memory_space=pltpu.VMEM),
        scratch_shapes=[
            pltpu.SMEM((sequences,), jnp.int32),
            vmem(query_low.shape, BF16),
            vmem((sequences, depth, LANES), F32),
            vmem(qw_shape, BF16),
            vmem(latent_cache.shape, BF16),
            vmem((own_heads, rank, v_dim), BF16),
            vmem(output_weight.shape, BF16),
            vmem((C, sequences, chunk), F32),
            vmem((C, sequences, chunk), F32),
            vmem((sequences, chunk), F32),
            vmem((sequences, own_heads, padded), F32),
            vmem((sequences, H, C, own_heads, padded), BF16),
            vmem((sequences, all_heads, padded), F32),
            vmem((sequences, all_heads, padded), F32),
            vmem((sequences * own_heads, rank), F32),
            vmem((sequences, C, H, own_heads, padded), BF16),
            vmem((sequences, C, H, own_heads, padded), BF16),
            vmem((sequences, H, own_heads, padded), F32),
            vmem((sequences, H, own_heads, padded), F32),
            vmem((sequences, own_heads * v_dim), F32),
            vmem((C, sequences, own_heads * v_dim), BF16),
            vmem((sequences, features), F32),
            vmem((H, sequences, share), F32),
            vmem((H, sequences, share), F32),
            dma((5,)),
            dma((C,)),
            dma((C,)),
            dma((C,)),
            dma((sequences, H)),
            dma((sequences, H)),
            dma((sequences, H, C)),
            dma((sequences, H, C)),
            dma((sequences, C)),
            dma((sequences, C)),
            dma((sequences, H)),
            dma((sequences, H)),
            dma((C,)),
            dma((C,)),
            dma((H,)),
            dma((H,)),
        ],
        compiler_params=pltpu.CompilerParams(
            collective_id=0, has_side_effects=True, vmem_limit_bytes=60 * 1024 * 1024
        ),
    )(lengths, query_low, query_weight, latent_cache, value_weight, output_weight)
    return result.astype(BF16)


def solution(mesh):
    return jax.shard_map(
        functools.partial(on_device, mesh.shape["ctx"], mesh.shape["head"]),
        mesh=mesh,
        in_specs=(
            P(None, "ctx"),
            P("ctx", "head"),
            P(None, ("ctx", "head"), None),
            P(),
            P("head", None, None),
            P("head", "ctx"),
        ),
        out_specs=P(None, ("ctx", "head")),
        check_vma=False,
    )
```

```python
import functools

import jax
import jax.numpy as jnp
from jax import lax
from jax.experimental import pallas as pl
from jax.experimental.pallas import tpu as pltpu
from jax.sharding import PartitionSpec as P

softmax_scale = 0.07216878
LANES = 128
F32 = jnp.float32
BF16 = jnp.bfloat16


def parts_of(x):
    high = x.astype(BF16).astype(F32)
    rest = x - high
    middle = rest.astype(BF16).astype(F32)
    return high, middle, rest - middle


def lane_sum(x, first, last):
    lane = lax.broadcasted_iota(jnp.int32, x.shape, x.ndim - 1)
    return jnp.sum(jnp.where((lane >= first) & (lane < last), x, 0.0), axis=-1, keepdims=True)


def kernel(
    ctx_count,
    head_count,
    lengths_from,
    query_low_from,
    query_weight,
    latent_cache,
    value_weight,
    output_weight,
    out,
    lengths,
    query_low,
    spread,
    qw,
    cache,
    vw,
    ow,
    partial,
    partial_in,
    summed,
    query_rows,
    gathered,
    queries,
    numer,
    latent_rows,
    stat_send,
    stat_in,
    plane_send,
    plane_in,
    value_rows,
    value_all,
    projected,
    out_send,
    out_in,
    load_sem,
    qw_sem,
    p_send,
    p_recv,
    gz_send,
    gz_recv,
    gc_send,
    gc_recv,
    s_send,
    s_recv,
    z_send,
    z_recv,
    v_send,
    v_recv,
    o_send,
    o_recv,
):
    C, H = ctx_count, head_count
    me_c, me_h = lax.axis_index("ctx"), lax.axis_index("head")
    sequences = query_low.shape[0]
    pieces, depth, _ = qw.shape
    chunk = partial.shape[2]
    own_heads = query_rows.shape[1]
    width, span = cache.shape[1], cache.shape[2]
    rank = vw.shape[1]
    v_dim = vw.shape[2]
    share = out.shape[1]

    def ctx_peer(step):
        return lax.rem(me_c + step, C)

    def head_peer(step):
        return lax.rem(me_h + step, H)

    def remote(source, target, send_sem, recv_sem, c, h):
        return pltpu.make_async_remote_copy(
            src_ref=source,
            dst_ref=target,
            send_sem=send_sem,
            recv_sem=recv_sem,
            device_id=(c, h),
            device_id_type=pl.DeviceIdType.MESH,
        )

    def loop(low, high, body):
        def run(i, carry):
            body(i)
            return carry

        lax.fori_loop(low, high, run, 0)

    def qw_copy(index):
        if pieces == 1:
            return pltpu.make_async_copy(query_weight, qw.at[0], qw_sem.at[0])
        columns = pl.ds(pl.multiple_of(index * chunk, LANES), chunk)
        return pltpu.make_async_copy(query_weight.at[:, columns], qw.at[index], qw_sem.at[index])

    barrier = pltpu.get_barrier_semaphore()

    def greet(c, h):
        pl.semaphore_signal(
            barrier, inc=1, device_id=(c, h), device_id_type=pl.DeviceIdType.MESH
        )

    loop(1, H, lambda o: greet(me_c, head_peer(o)))
    loop(1, C, lambda o: greet(ctx_peer(o), me_h))

    lengths_copy = pltpu.make_async_copy(lengths_from, lengths, load_sem.at[3])
    low_copy = pltpu.make_async_copy(query_low_from, query_low, load_sem.at[4])
    low_copy.start()
    lengths_copy.start()
    if pieces == 1:
        qw_copy(0).start()
    else:
        loop(1, C + 1, lambda o: qw_copy(ctx_peer(o)).start())
    cache_copy = pltpu.make_async_copy(latent_cache, cache, load_sem.at[0])
    vw_copy = pltpu.make_async_copy(
        value_weight.at[pl.ds(me_c * own_heads, own_heads)], vw, load_sem.at[1]
    )
    ow_copy = pltpu.make_async_copy(output_weight, ow, load_sem.at[2])

    low_copy.wait()
    for b in range(sequences):
        pick = lax.broadcasted_iota(jnp.int32, (sequences, LANES), 0) == b
        spread[b] = lax.dot_general(
            query_low[...],
            jnp.where(pick, 1.0, 0.0).astype(BF16),
            (((0,), (0,)), ((), ())),
            preferred_element_type=F32,
        )

    def p_copy(o):
        c = ctx_peer(o)
        return remote(
            partial.at[c], partial_in.at[me_c], p_send.at[o], p_recv.at[me_c], c, me_h
        )

    def multiply(index):
        qw_copy(index).wait()
        for at in range(0, chunk, LANES):
            weight = qw[index, :, at : at + LANES].astype(F32)
            for b in range(sequences):
                partial[index, b : b + 1, at : at + LANES] = jnp.sum(
                    weight * spread[b], axis=0, keepdims=True
                )

    if pieces == 1:
        qw_copy(0).wait()
        for c in range(C):
            partial[c] = jnp.dot(
                query_low[...], qw[0, :, c * chunk : (c + 1) * chunk], preferred_element_type=F32
            )
        pl.semaphore_wait(barrier, C + H - 2)
        loop(1, C, lambda o: p_copy(o).start())
    else:

        def send_partial(o):
            p_copy(o).start()
            multiply(ctx_peer(o + 1))

        multiply(ctx_peer(1))
        pl.semaphore_wait(barrier, C + H - 2)
        loop(1, C, send_partial)
    cache_copy.start()
    vw_copy.start()
    ow_copy.start()
    query_rows[...] = jnp.zeros_like(query_rows)
    partial_in[me_c] = partial[me_c]

    def p_wait(o):
        c = ctx_peer(o)
        remote(partial.at[c], partial_in.at[c], p_send.at[o], p_recv.at[c], c, me_h).wait_recv()

    loop(1, C, p_wait)
    total = partial_in[0]
    for c in range(1, C):
        total = total + partial_in[c]
    summed[...] = total
    for b in range(sequences):
        for j in range(own_heads):
            query_rows[b, j : j + 1, 0:width] = summed[b : b + 1, j * width : (j + 1) * width]
        gathered[me_h, me_c, b] = query_rows[b].astype(BF16)

    def gz_copy(o):
        h = head_peer(o)
        slot = gathered.at[me_h, me_c]
        return remote(slot, slot, gz_send.at[o], gz_recv.at[me_h], me_c, h)

    def gc_copy(step, o):
        h = head_peer(step)
        slot = gathered.at[h, me_c]
        return remote(
            slot, slot, gc_send.at[step, o], gc_recv.at[h, me_c], ctx_peer(o), me_h
        )

    def forward(step):
        h = head_peer(step)
        slot = gathered.at[h, me_c]
        remote(slot, slot, gz_send.at[step], gz_recv.at[h], me_c, h).wait_recv()
        loop(1, C, lambda o: gc_copy(step, o).start())

    def gc_wait(step):
        def one(o):
            h, c = head_peer(step), ctx_peer(o)
            slot = gathered.at[h, c]
            remote(slot, slot, gc_send.at[step, o], gc_recv.at[h, c], c, me_h).wait_recv()

        loop(1, C, one)

    loop(1, H, lambda o: gz_copy(o).start())
    loop(1, C, lambda o: gc_copy(0, o).start())
    loop(1, H, lambda step: forward(step))
    cache_copy.wait()

    def s_copy(b, o):
        c = ctx_peer(o)
        return remote(
            stat_send.at[b, c], stat_in.at[b, me_c], s_send.at[b, o], s_recv.at[b, me_c], c, me_h
        )

    lengths_copy.wait()
    offset = (me_c * H + me_h) * span
    all_heads = queries.shape[1]
    loop(0, H, lambda step: gc_wait(step))
    for b in range(sequences):
        for h in range(H):
            for c in range(C):
                first = (h * C + c) * own_heads
                queries[b, first : first + own_heads, :] = gathered[h, c, b].astype(F32)
        usable = (
            offset + lax.broadcasted_iota(jnp.int32, (all_heads, span), 1)
        ) < lengths[b]
        scores = (
            jnp.dot(
                queries[b, :, 0:width].astype(BF16), cache[b], preferred_element_type=F32
            )
            * softmax_scale
        )
        scores = jnp.where(usable, scores, -1e30)
        local_max = jnp.max(scores, axis=1, keepdims=True)
        probabilities = jnp.where(usable, jnp.exp(scores - local_max), 0.0)
        totals = jnp.sum(probabilities, axis=1, keepdims=True)
        numer[b, :, 0:rank] = lax.dot_general(
            probabilities.astype(BF16),
            cache[b, 0:rank, :],
            (((1,), (1,)), ((), ())),
            preferred_element_type=F32,
        )
        lane = lax.broadcasted_iota(jnp.int32, (all_heads, LANES), 1)
        extra = jnp.zeros((all_heads, LANES), F32)
        for at, part in enumerate(parts_of(local_max) + parts_of(totals)):
            extra = jnp.where(lane == at, part, extra)
        numer[b, :, rank:] = extra
        for h in range(H):
            for c in range(C):
                first = (h * C + c) * own_heads
                stat_send[b, c, h] = numer[b, first : first + own_heads, :].astype(BF16)
        loop(1, C, lambda o: s_copy(b, o).start())
        stat_in[b, me_c] = stat_send[b, me_c]

    def s_wait(b, o):
        c = ctx_peer(o)
        remote(
            stat_send.at[b, c], stat_in.at[b, c], s_send.at[b, o], s_recv.at[b, c], c, me_h
        ).wait_recv()

    def z_copy(b, o):
        h = head_peer(o)
        return remote(
            plane_send.at[b, h], plane_in.at[b, me_h], z_send.at[b, o], z_recv.at[b, me_h], me_c, h
        )

    def z_wait(b, o):
        h = head_peer(o)
        remote(
            plane_send.at[b, h], plane_in.at[b, h], z_send.at[b, o], z_recv.at[b, h], me_c, h
        ).wait_recv()

    for b in range(sequences):
        loop(1, C, lambda o: s_wait(b, o))
        maxima, sums = [], []
        for c in range(C):
            extra = stat_in[b, c, :, :, rank:].astype(F32)
            maxima.append(lane_sum(extra, 0, 3))
            sums.append(lane_sum(extra, 3, 6))
        highest = functools.reduce(jnp.maximum, maxima)
        total, weighted = 0.0, 0.0
        for c in range(C):
            scale = jnp.exp(maxima[c] - highest)
            total = total + sums[c] * scale
            weighted = weighted + stat_in[b, c, :, :, 0:rank].astype(F32) * scale
        lane = lax.broadcasted_iota(jnp.int32, (H, own_heads, LANES), 2)
        plane_send[b, :, :, 0:rank] = weighted
        plane_send[b, :, :, rank:] = jnp.where(
            lane == 0, highest, jnp.where(lane == 1, total, 0.0)
        )
        loop(1, H, lambda o: z_copy(b, o).start())
        plane_in[b, me_h] = plane_send[b, me_h]
    for b in range(sequences):
        loop(1, H, lambda o: z_wait(b, o))
        maxima, sums = [], []
        for h in range(H):
            extra = plane_in[b, h, :, rank:]
            maxima.append(lane_sum(extra, 0, 1))
            sums.append(lane_sum(extra, 1, 2))
        highest = functools.reduce(jnp.maximum, maxima)
        total, weighted = 0.0, 0.0
        for h in range(H):
            scale = jnp.exp(maxima[h] - highest)
            total = total + sums[h] * scale
            weighted = weighted + plane_in[b, h, :, 0:rank] * scale
        latent_rows[b * own_heads : (b + 1) * own_heads, :] = weighted / total
    latent_out = latent_rows[...].astype(BF16)

    vw_copy.wait()
    for j in range(own_heads):
        value = jnp.dot(latent_out, vw[j], preferred_element_type=F32)
        for b in range(sequences):
            row = b * own_heads + j
            value_rows[b : b + 1, j * v_dim : (j + 1) * v_dim] = value[row : row + 1, :]
    value_all[me_c] = value_rows[...].astype(BF16)

    def v_copy(o):
        slot = value_all.at[me_c]
        return remote(slot, slot, v_send.at[o], v_recv.at[me_c], ctx_peer(o), me_h)

    loop(1, C, lambda o: v_copy(o).start())

    def v_wait(o):
        c = ctx_peer(o)
        slot = value_all.at[c]
        remote(slot, slot, v_send.at[o], v_recv.at[c], c, me_h).wait_recv()

    ow_copy.wait()
    block_rows = own_heads * v_dim
    projected[...] = jnp.zeros_like(projected)

    def project(c):
        at = pl.ds(pl.multiple_of(c * block_rows, block_rows), block_rows)
        projected[...] += jnp.dot(value_all[c], ow[at, :], preferred_element_type=F32)

    def project_next(o):
        v_wait(o)
        project(ctx_peer(o))

    project(me_c)
    loop(1, C, project_next)
    for h in range(H):
        out_send[h] = projected[:, h * share : (h + 1) * share]

    def o_copy(o):
        h = head_peer(o)
        return remote(out_send.at[h], out_in.at[me_h], o_send.at[o], o_recv.at[me_h], me_c, h)

    loop(1, H, lambda o: o_copy(o).start())
    out_in[me_h] = out_send[me_h]

    def o_wait(o):
        h = head_peer(o)
        remote(out_send.at[h], out_in.at[h], o_send.at[o], o_recv.at[h], me_c, h).wait_recv()

    loop(1, H, o_wait)
    result = out_in[0]
    for h in range(1, H):
        result = result + out_in[h]
    out[...] = result

    loop(1, C, lambda o: p_copy(o).wait_send())
    loop(1, H, lambda o: gz_copy(o).wait_send())
    loop(0, H, lambda step: loop(1, C, lambda o: gc_copy(step, o).wait_send()))
    for b in range(sequences):
        loop(1, C, lambda o: s_copy(b, o).wait_send())
        loop(1, H, lambda o: z_copy(b, o).wait_send())
    loop(1, C, lambda o: v_copy(o).wait_send())
    loop(1, H, lambda o: o_copy(o).wait_send())


def on_device(
    C, H, query_low, query_weight, latent_cache, lengths, value_weight, output_weight
):
    latent_cache = jnp.swapaxes(latent_cache, 1, 2)
    sequences = query_low.shape[0]
    local_heads, rank, v_dim = value_weight.shape
    depth, columns = query_weight.shape
    own_heads = local_heads // C
    chunk = columns // C
    all_heads = local_heads * H
    padded = rank + LANES
    features = output_weight.shape[1]
    share = features // H
    qw_shape = (C, depth, chunk) if chunk % LANES == 0 else (1, depth, columns)
    vmem, dma = pltpu.VMEM, pltpu.SemaphoreType.DMA
    result = pl.pallas_call(
        functools.partial(kernel, C, H),
        out_shape=jax.ShapeDtypeStruct((sequences, share), F32),
        in_specs=[
            pl.BlockSpec(memory_space=pltpu.HBM),
            pl.BlockSpec(memory_space=pltpu.HBM),
            pl.BlockSpec(memory_space=pltpu.HBM),
            pl.BlockSpec(memory_space=pltpu.HBM),
            pl.BlockSpec(memory_space=pltpu.HBM),
            pl.BlockSpec(memory_space=pltpu.HBM),
        ],
        out_specs=pl.BlockSpec(memory_space=pltpu.VMEM),
        scratch_shapes=[
            pltpu.SMEM((sequences,), jnp.int32),
            vmem(query_low.shape, BF16),
            vmem((sequences, depth, LANES), F32),
            vmem(qw_shape, BF16),
            vmem(latent_cache.shape, BF16),
            vmem((own_heads, rank, v_dim), BF16),
            vmem(output_weight.shape, BF16),
            vmem((C, sequences, chunk), F32),
            vmem((C, sequences, chunk), F32),
            vmem((sequences, chunk), F32),
            vmem((sequences, own_heads, padded), F32),
            vmem((H, C, sequences, own_heads, padded), BF16),
            vmem((sequences, all_heads, padded), F32),
            vmem((sequences, all_heads, padded), F32),
            vmem((sequences * own_heads, rank), F32),
            vmem((sequences, C, H, own_heads, padded), BF16),
            vmem((sequences, C, H, own_heads, padded), BF16),
            vmem((sequences, H, own_heads, padded), F32),
            vmem((sequences, H, own_heads, padded), F32),
            vmem((sequences, own_heads * v_dim), F32),
            vmem((C, sequences, own_heads * v_dim), BF16),
            vmem((sequences, features), F32),
            vmem((H, sequences, share), F32),
            vmem((H, sequences, share), F32),
            dma((5,)),
            dma((C,)),
            dma((C,)),
            dma((C,)),
            dma((H,)),
            dma((H,)),
            dma((H, C)),
            dma((H, C)),
            dma((sequences, C)),
            dma((sequences, C)),
            dma((sequences, H)),
            dma((sequences, H)),
            dma((C,)),
            dma((C,)),
            dma((H,)),
            dma((H,)),
        ],
        compiler_params=pltpu.CompilerParams(
            collective_id=0, has_side_effects=True, vmem_limit_bytes=60 * 1024 * 1024
        ),
    )(lengths, query_low, query_weight, latent_cache, value_weight, output_weight)
    return result.astype(BF16)


def solution(mesh):
    return jax.shard_map(
        functools.partial(on_device, mesh.shape["ctx"], mesh.shape["head"]),
        mesh=mesh,
        in_specs=(
            P(None, "ctx"),
            P("ctx", "head"),
            P(None, ("ctx", "head"), None),
            P(),
            P("head", None, None),
            P("head", "ctx"),
        ),
        out_specs=P(None, ("ctx", "head")),
        check_vma=False,
    )
```
